768 devices in a mesh: segment: 16 (over y, core), dp: 3 (over z_hi), expert: 16 (over x, z_lo).
Axes of the slice: x: 4, y: 8, z: 12 (z_hi: 3, z_lo: 4; z = z_hi * 4 + z_lo), core: 2. Of those that a mesh axis runs over, the one named last changes fastest.
Arguments:
- saved_b: bfloat16 [16, 6144, 2048], P('segment', ('dp', 'expert')), may hold values from -6 to 6
- route_b: int32 [16, 6144, 1], P('segment', ('dp', 'expert')), may hold values from 0 to 15; in each aligned block of 128 rows (0 to 127, 128 to 255, ..., all dimensions but the last counted through in order) at most 10 rows name the same one
- gate_b: float32 [16, 6144, 1], P('segment', ('dp', 'expert')), may hold values from 0.2 to 1
- grad_y_b: bfloat16 [16, 6144, 2048], P('segment', ('dp', 'expert')), may hold values from -6 to 6
- w_in: bfloat16 [16, 16, 2048, 768], P('segment', 'expert'), may hold values from -0.125 to 0.125
- w_out: bfloat16 [16, 16, 768, 2048], P('segment', 'expert'), may hold values from -0.21875 to 0.21875
Outputs:
- grad_x_b: bfloat16 [16, 6144, 2048], P('segment', ('dp', 'expert'))
- grad_in: bfloat16 [16, 16, 2048, 768], P('segment', 'expert', None, 'dp')
The draws below stay inside these ranges and needn't reach their ends.
Inputs may be any that keep to these rules, and one draw needn't show every extreme that they name: `route_b`: of the 128 tokens of one device of a section, at most 10 pick any one expert; some device sends exactly 10 to some expert.
All inputs are finite; a program needn't handle non-finite values.
Results may differ from the reference program's by a relative error of at most 0.01.
Values may be sent and summed in bfloat16 or wider, within the bound.
No kernel may reach another device: no remote copies, remote signals or barrier semaphores. Data moves between devices by JAX's collectives and lax.ppermute only.
A program may use at most 64 MiB of HBM per device.

```python
import math
import jax
import jax.numpy as jnp
import numpy as np
from jax import lax

D = 2048
F = 768
TOK_DEV = 128
N_EXP_ALL = 16
CAP = 10
TOKENS = 6144
N_SEGMENT = 16
N_DP = 3
N_EXPERT = 16


def levels(rng, shape, cuts, low, high):
    gain, own = 1.0, jax.random.fold_in(rng, 6)
    for dim, parts in cuts:
        draws = jnp.exp(jax.random.uniform(jax.random.fold_in(own, dim), (parts,), jnp.float32, low / len(cuts), high / len(cuts)))
        gain = gain * jnp.repeat(draws, shape[dim] // parts).reshape([-1 if axis == dim else 1 for axis in range(len(shape))])
    return gain


def shared_out(own_key, own, number, rows, number_of, top, most, slope):
    ranking = jax.random.permutation(own_key, number_of)
    heavy_load, ordinary = portions_of(number_of, rows * top, most, slope, True), portions_of(number_of, rows * top, most, slope, False)
    places = jnp.arange(number_of)

    def named(sizes, rotation):
        used = int((sizes > 0).sum())
        fixed = max(1, used // 4)
        passed = fixed + (places - fixed + rotation * (used - fixed)) % max(1, number_of - fixed)
        return jnp.zeros((number_of,), jnp.int32).at[ranking[jnp.where(places < fixed, places, passed)]].set(jnp.asarray(sizes, jnp.int32))

    sizes = jnp.where(number % 4 == 0, named(heavy_load, number // 4), named(ordinary, number - number // 4 - 1))
    mixed = jax.random.permutation(jax.random.fold_in(own, 3), number_of)
    source_of, sink = mixed[0:number_of // 2 * 2:2], mixed[1:number_of // 2 * 2:2]
    room = jnp.minimum(sizes[source_of] - 1, most - sizes[sink]) // 2
    room = jnp.where((source_of == ranking[0]) | (sink == ranking[0]) | (sizes[sink] == 0), 0, jnp.maximum(room, 0))
    passed = jax.random.randint(jax.random.fold_in(own, 4), (number_of // 2,), 0, 1 << 20) % (room + 1)
    sizes = sizes.at[source_of].add(-passed).at[sink].add(passed)
    labels = jnp.searchsorted(jnp.cumsum(sizes), jnp.arange(rows * top), side="right").astype(jnp.int32)
    table = labels.reshape(top, rows).T
    table = table[jax.random.permutation(jax.random.fold_in(own, 1), rows)]
    rotation = jax.random.randint(jax.random.fold_in(own, 2), (rows, 1), 0, top)
    return jnp.take_along_axis(table, (jnp.arange(top)[None, :] + rotation) % top, axis=1)


def portions_of(number_of, total, bound, skew, full):
    loads = [(1 << 20) // math.isqrt(grade ** skew) + 1 for grade in range(1, number_of + 1)]
    largest = bound if full else min(bound, max(-(-total // number_of), total * loads[0] // sum(loads)))
    least = 1 if total - largest >= number_of - 1 else 0
    given, rest = [largest] + [least] * (number_of - 1), total - largest - least * (number_of - 1)
    while rest > 0:
        candidates = [i for i in range(1, number_of) if given[i] < largest] or [i for i in range(1, number_of) if given[i] < bound]
        whole, left = sum([loads[i] for i in candidates]), rest
        for i in candidates:
            more = min(bound - given[i], max(1, left * loads[i] // whole), rest)
            given[i] = given[i] + more
            rest = rest - more
    return np.array(given)


def bell_draw(rng, shape, spread, reach, cuts=(), kind=jnp.bfloat16):
    entries = spread * jax.random.normal(rng, shape, jnp.float32)
    if cuts:
        entries = entries * levels(rng, shape, cuts, -0.22, 0.18)
    return jnp.clip(entries, -reach, reach).astype(kind)


def setup_inputs(seed: int = 0) -> dict:
    seeds = jax.random.split(jax.random.key(seed), 7)
    saved_b = bell_draw(seeds[0], (N_SEGMENT, TOKENS, D), 1.0, 6.0, ((0, 16), (1, 48)))
    route_b_keys = jax.random.split(jax.random.fold_in(seeds[1], 1), N_SEGMENT * TOKENS // TOK_DEV)
    route_b_turns = jax.random.permutation(jax.random.fold_in(seeds[1], 3), N_SEGMENT * TOKENS // TOK_DEV)
    route_b = jax.vmap(lambda own, number: shared_out(jax.random.fold_in(seeds[1], 2), own, number, TOK_DEV, N_EXPERT, 1, CAP, 2))(route_b_keys, route_b_turns).reshape((N_SEGMENT, TOKENS, 1))
    gate_b = jnp.clip(0.2 + 0.8 * jax.random.uniform(seeds[2], (N_SEGMENT, TOKENS, 1), jnp.float32) ** levels(seeds[2], (N_SEGMENT, TOKENS, 1), ((0, 16), (1, 48)), -0.2, 0.2), 0.2, 1.0)
    grad_y_b = bell_draw(seeds[3], (N_SEGMENT, TOKENS, D), 1.0, 6.0, ((0, 16), (1, 48)))
    w_in = bell_draw(seeds[4], (N_SEGMENT, N_EXP_ALL, D, F), D ** -0.5, 0.125, ((0, 16), (1, 16)))
    w_out = bell_draw(seeds[5], (N_SEGMENT, N_EXP_ALL, F, D), F ** -0.5, 0.21875, ((0, 16), (1, 16)))
    return {"saved_b": saved_b, "route_b": route_b, "gate_b": gate_b, "grad_y_b": grad_y_b, "w_in": w_in, "w_out": w_out}


def silu_grad(value):
    sigma = jax.nn.sigmoid(value)
    return sigma * (1.0 + value * (1.0 - sigma))

def positions(route):
    expert_ids = route[..., 0]
    onehot = (expert_ids[..., None] == jnp.arange(N_EXPERT, dtype=jnp.int32)).astype(jnp.int32)
    before = jnp.cumsum(onehot, axis=1) - onehot
    return (expert_ids * CAP + lax.optimization_barrier(jnp.sum(before * onehot, axis=2))).astype(jnp.int32)

def fill_one(buffer, position, values):
    return buffer.at[position].set(values)

def read_one(buffer, position):
    return buffer[position]

def to_slots(values, position):
    devices = values.shape[0]
    empty = jnp.zeros((devices, N_EXPERT * CAP, D), values.dtype)
    filled = jax.vmap(fill_one)(empty, position, values)
    return filled.reshape(devices, N_EXPERT, CAP, D).transpose(1, 0, 2, 3).reshape(N_EXPERT, devices * CAP, D)

def from_slots(rows, position):
    devices = position.shape[0]
    grouped = rows.reshape(N_EXPERT, devices, CAP, D).transpose(1, 0, 2, 3).reshape(devices, N_EXPERT * CAP, D)
    return jax.vmap(read_one)(grouped, position)

def section(pack):
    saved_b, route_b, gate_b, cotangent, w_in, w_out = pack
    devices = N_DP * N_EXPERT
    shape_rows = (devices, TOK_DEV, D)
    weight_in = w_in.astype(jnp.float32)
    weight_out = w_out.astype(jnp.float32)
    scaled = (gate_b.reshape(devices, TOK_DEV, 1) * cotangent.reshape(shape_rows).astype(jnp.float32)).astype(jnp.bfloat16)
    pos_b = positions(route_b.reshape(devices, TOK_DEV, 1))
    slots_x = to_slots(saved_b.reshape(shape_rows), pos_b).astype(jnp.float32)
    slots_g = to_slots(scaled, pos_b).astype(jnp.float32)
    pre_b = jnp.einsum('erd,edf->erf', slots_x, weight_in)
    grad_h = jnp.einsum('erd,efd->erf', slots_g, weight_out)
    grad_pre = (grad_h * silu_grad(pre_b)).astype(jnp.bfloat16)
    grad_slots = jnp.einsum('erf,edf->erd', grad_pre.astype(jnp.float32), weight_in).astype(jnp.bfloat16)
    grad_x = from_slots(grad_slots, pos_b)
    group_rows = N_EXPERT * CAP
    group_x = slots_x.reshape(N_EXPERT, N_DP, group_rows, D)
    group_pre = grad_pre.astype(jnp.float32).reshape(N_EXPERT, N_DP, group_rows, F)
    part_in = jnp.einsum('egrd,egrf->egdf', group_x, group_pre).astype(jnp.bfloat16)
    part_in = lax.optimization_barrier(part_in)
    grad_in = lax.optimization_barrier(jnp.sum(part_in.astype(jnp.float32), axis=1)).astype(jnp.bfloat16)
    return (grad_x.reshape(TOKENS, D), grad_in)

def reference(saved_b, route_b, gate_b, grad_y_b, w_in, w_out):
    arrived = jnp.roll(grad_y_b, -1, axis=0)
    results = lax.map(section, (saved_b, route_b, gate_b, arrived, w_in, w_out))
    return (results[0], results[1])
```

```python
import functools

import jax
import jax.numpy as jnp
from jax import lax
from jax.experimental import pallas as pl
from jax.experimental.pallas import tpu as pltpu
from jax.sharding import PartitionSpec as P

PIECES = 4
F32 = jnp.float32
BF16 = jnp.bfloat16


def passed_along(value, axis, steps):
    count = lax.axis_size(axis)
    pairs = [(source, (source + steps) % count) for source in range(count)]
    return lax.ppermute(value, axis, pairs)


def silu_grad(value):
    sigma = jax.nn.sigmoid(value)
    return sigma * (1.0 + value * (1.0 - sigma))


def iota(shape, dim):
    return lax.broadcasted_iota(jnp.int32, shape, dim)


def one_hot(condition):
    return jnp.where(condition, 1.0, 0.0).astype(BF16)


def dot(a, b, contract=((1,), (0,))):
    return lax.dot_general(a, b, (contract, ((), ())), preferred_element_type=F32)


def slots_along_lanes(route, experts, capacity):
    tokens = route.shape[0]
    square = (tokens, tokens)
    lane_route = jnp.sum(
        jnp.where(iota(square, 0) == iota(square, 1), route.astype(F32), 0.0), axis=0, keepdims=True
    )
    named = one_hot(iota((experts, tokens), 0).astype(F32) == lane_route)
    before = dot(named, one_hot(iota(square, 0) < iota(square, 1)))
    rank = jnp.sum(before * named.astype(F32), axis=0, keepdims=True)
    return (lane_route * (PIECES * capacity) + rank).astype(jnp.int32)


def slots_along_sublanes(route, capacity):
    tokens = route.shape[0]
    square = (tokens, tokens)
    named = one_hot(iota(square, 1) == route)
    before = dot(one_hot(iota(square, 1) < iota(square, 0)), named)
    rank = jnp.sum(before * named.astype(F32), axis=1, keepdims=True)
    return route * (PIECES * capacity) + rank.astype(jnp.int32)


def place(slot, values, capacity, rows):
    tokens, width = values.shape
    short = width // PIECES
    at = iota((rows, tokens), 0)
    table = jnp.concatenate([one_hot(at == slot + p * capacity) for p in range(PIECES)], axis=1)
    stacked = jnp.concatenate([values[:, p * short : (p + 1) * short] for p in range(PIECES)], axis=0)
    return dot(table, stacked).astype(BF16)


def dispatch_x_kernel(capacity, experts, route_ref, values_ref, out_ref):
    slot = slots_along_lanes(route_ref[...], experts, capacity)
    out_ref[...] = place(slot, values_ref[...], capacity, out_ref.shape[0])


def dispatch_g_kernel(capacity, experts, route_ref, gate_ref, values_ref, out_ref):
    slot = slots_along_lanes(route_ref[...], experts, capacity)
    scaled = (gate_ref[...] * values_ref[...].astype(F32)).astype(BF16)
    out_ref[...] = place(slot, scaled, capacity, out_ref.shape[0])


def combine_kernel(capacity, route_ref, rows_ref, out_ref):
    slot = slots_along_sublanes(route_ref[...], capacity)
    rows = rows_ref[...]
    count, short = rows.shape
    at = iota((slot.shape[0], count), 1)
    for p in range(PIECES):
        table = one_hot(at == slot + p * capacity)
        out_ref[:, p * short : (p + 1) * short] = dot(table, rows).astype(BF16)


def short_row(capacity, row, piece):
    group = (row * (65536 // capacity + 1)) >> 16
    return row + group * ((PIECES - 1) * capacity) + piece * capacity


def whole_piece(capacity, rows, piece):
    count = rows.shape[0]
    shape = (count // PIECES, count)
    pick = one_hot(iota(shape, 1) == short_row(capacity, iota(shape, 0), piece))
    return dot(pick, rows).astype(BF16)


def pre_kernel(capacity, rows_ref, w_in_ref, pre_ref):
    rows = rows_ref[...]
    short = rows.shape[1]
    total = None
    for p in range(PIECES):
        term = dot(whole_piece(capacity, rows, p), w_in_ref[p * short : (p + 1) * short, :])
        total = term if total is None else total + term
    pre_ref[...] = total


def expert_kernel(capacity, parts, place_ref, rows_ref, pre_ref, w_in_ref, w_out_ref,
                  back_ref, own_ref, up_ref, down_ref, hold_ref):
    rows = rows_ref[...]
    count, short = rows.shape
    total = None
    for p in range(PIECES):
        term = dot(whole_piece(capacity, rows, p), w_out_ref[:, p * short : (p + 1) * short], ((1,), (1,)))
        total = term if total is None else total + term
    grad_pre = (total * silu_grad(pre_ref[...])).astype(BF16)
    hold_ref[...] = grad_pre
    shape = (count, count // PIECES)
    back = None
    for p in range(PIECES):
        piece = dot(grad_pre, w_in_ref[p * short : (p + 1) * short, :], ((1,), (1,))).astype(BF16)
        put = one_hot(iota(shape, 0) == short_row(capacity, iota(shape, 1), p))
        term = dot(put, piece)
        back = term if back is None else back + term
    back_ref[...] = back.astype(BF16)
    width = own_ref.shape[1]
    me = place_ref[0]
    for ref, step in ((own_ref, 0), (up_ref, 1), (down_ref, parts - 1)):
        part = lax.rem(me + step, parts)
        ref[...] = hold_ref[:, pl.ds(pl.multiple_of(part * width, width), width)]


def weight_kernel(capacity, *refs):
    out_ref = refs[-1]
    half = (len(refs) - 1) // 2
    short = refs[0].shape[1]
    for p in range(PIECES):
        total = None
        for rows_ref, grad_ref in zip(refs[:half], refs[half:-1], strict=True):
            term = dot(whole_piece(capacity, rows_ref[...], p), grad_ref[...], ((0,), (0,)))
            total = term if total is None else total + term
        out_ref[p * short : (p + 1) * short, :] = total.astype(BF16)


VMEM = pl.BlockSpec(memory_space=pltpu.VMEM)
SMEM = pl.BlockSpec(memory_space=pltpu.SMEM)


def call(kernel, outs, args, specs=None, scratch=(), flops=10**9, moved=4 * 10**6):
    many = isinstance(outs, tuple)
    return pl.pallas_call(
        kernel,
        out_shape=outs,
        in_specs=specs or [VMEM] * len(args),
        out_specs=(VMEM,) * len(outs) if many else VMEM,
        scratch_shapes=list(scratch),
        compiler_params=pltpu.CompilerParams(vmem_limit_bytes=40 * 2**20),
        cost_estimate=pl.CostEstimate(flops=flops, bytes_accessed=moved, transcendentals=0),
    )(*args)


def body(saved_b, route_b, gate_b, grad_y_b, w_in, w_out):
    experts = lax.axis_size("expert")
    parts = lax.axis_size("dp")
    tokens, width = saved_b.shape[1:]
    hidden = w_in.shape[3]
    capacity = max(2, tokens * 5 // (4 * experts))
    count, short = experts * capacity * PIECES, width // PIECES
    table = jax.ShapeDtypeStruct((count, short), BF16)
    route, weight_in, weight_out = route_b[0], w_in[0, 0], w_out[0, 0]

    def exchange(rows):
        return lax.all_to_all(rows, "expert", split_axis=0, concat_axis=0, tiled=True)

    arrived = passed_along(grad_y_b, "segment", -1)[0]
    send_x = call(functools.partial(dispatch_x_kernel, capacity, experts), table, (route, saved_b[0]))
    recv_x = exchange(send_x)
    send_g = call(functools.partial(dispatch_g_kernel, capacity, experts), table, (route, gate_b[0], arrived))
    recv_g = exchange(send_g)
    x_from_below = passed_along(recv_x, "dp", 1)
    x_from_above = passed_along(recv_x, "dp", -1)
    pre = call(
        functools.partial(pre_kernel, capacity),
        jax.ShapeDtypeStruct((experts * capacity, hidden), F32),
        (recv_x, weight_in),
    )
    slim = jax.ShapeDtypeStruct((experts * capacity, hidden // parts), BF16)
    me = lax.axis_index("dp").astype(jnp.int32).reshape(1)
    back, own, up, down = call(
        functools.partial(expert_kernel, capacity, parts),
        (table, slim, slim, slim),
        (me, recv_g, pre, weight_in, weight_out),
        specs=[SMEM] + [VMEM] * 4,
        scratch=[pltpu.VMEM((experts * capacity, hidden), BF16)],
    )
    home = exchange(back)
    g_from_below = passed_along(up, "dp", 1)
    g_from_above = passed_along(down, "dp", -1)
    grad_x = call(
        functools.partial(combine_kernel, capacity),
        jax.ShapeDtypeStruct((tokens, width), BF16),
        (route, home),
    )
    grad_in = call(
        functools.partial(weight_kernel, capacity),
        jax.ShapeDtypeStruct((width, hidden // parts), BF16),
        (recv_x, x_from_below, x_from_above, own, g_from_below, g_from_above),
    )
    return (grad_x[None], grad_in[None, None])


def solution(mesh):
    return jax.shard_map(
        body,
        mesh=mesh,
        in_specs=(
            P("segment", ("dp", "expert"), None),
            P("segment", ("dp", "expert"), None),
            P("segment", ("dp", "expert"), None),
            P("segment", ("dp", "expert"), None),
            P("segment", "expert", None, None),
            P("segment", "expert", None, None),
        ),
        out_specs=(P("segment", ("dp", "expert"), None), P("segment", "expert", None, "dp")),
        check_vma=False,
    )
```

```python
import functools

import jax
import jax.numpy as jnp
from jax import lax
from jax.experimental import pallas as pl
from jax.experimental.pallas import tpu as pltpu
from jax.sharding import PartitionSpec as P

PIECES = 4
F32 = jnp.float32
BF16 = jnp.bfloat16


def passed_along(value, axis, steps):
    count = lax.axis_size(axis)
    pairs = [(source, (source + steps) % count) for source in range(count)]
    return lax.ppermute(value, axis, pairs)


def silu_grad(value):
    sigma = jax.nn.sigmoid(value)
    return sigma * (1.0 + value * (1.0 - sigma))


def iota(shape, dim):
    return lax.broadcasted_iota(jnp.int32, shape, dim)


def one_hot(condition):
    return jnp.where(condition, 1.0, 0.0).astype(BF16)


def dot(a, b, contract=((1,), (0,))):
    return lax.dot_general(a, b, (contract, ((), ())), preferred_element_type=F32)


def first_short_row(route, rank, capacity, piece):
    main = capacity // 8 * 8
    rest = capacity - main
    inside = jnp.where(rank < main, piece * main + rank, PIECES * main + piece * rest + rank - main)
    return route * (PIECES * capacity) + inside


def slots_along_lanes(route, experts):
    tokens = route.shape[0]
    square = (tokens, tokens)
    lane_route = jnp.sum(
        jnp.where(iota(square, 0) == iota(square, 1), route.astype(F32), 0.0), axis=0, keepdims=True
    )
    named = one_hot(iota((experts, tokens), 0).astype(F32) == lane_route)
    before = dot(named, one_hot(iota(square, 0) < iota(square, 1)))
    rank = jnp.sum(before * named.astype(F32), axis=0, keepdims=True)
    return lane_route.astype(jnp.int32), rank.astype(jnp.int32)


def slots_along_sublanes(route):
    tokens = route.shape[0]
    square = (tokens, tokens)
    named = one_hot(iota(square, 1) == route)
    before = dot(one_hot(iota(square, 1) < iota(square, 0)), named)
    return jnp.sum(before * named.astype(F32), axis=1, keepdims=True).astype(jnp.int32)


def place(route, values, capacity, experts, rows):
    tokens, width = values.shape
    short = width // PIECES
    lane_route, rank = slots_along_lanes(route, experts)
    at = iota((rows, tokens), 0)
    table = jnp.concatenate(
        [one_hot(at == first_short_row(lane_route, rank, capacity, p)) for p in range(PIECES)], axis=1
    )
    stacked = jnp.concatenate([values[:, p * short : (p + 1) * short] for p in range(PIECES)], axis=0)
    return dot(table, stacked).astype(BF16)


def dispatch_x_kernel(capacity, experts, route_ref, values_ref, out_ref):
    out_ref[...] = place(route_ref[...], values_ref[...], capacity, experts, out_ref.shape[0])


def dispatch_g_kernel(capacity, experts, route_ref, gate_ref, values_ref, out_ref):
    scaled = (gate_ref[...] * values_ref[...].astype(F32)).astype(BF16)
    out_ref[...] = place(route_ref[...], scaled, capacity, experts, out_ref.shape[0])


def combine_kernel(capacity, route_ref, rows_ref, _after_ref, out_ref):
    route = route_ref[...]
    rank = slots_along_sublanes(route)
    rows = rows_ref[...]
    count, short = rows.shape
    at = iota((route.shape[0], count), 1)
    for p in range(PIECES):
        table = one_hot(at == first_short_row(route, rank, capacity, p))
        out_ref[:, p * short : (p + 1) * short] = dot(table, rows).astype(BF16)


def rest_table(chunks, rest, piece, dim):
    long, slim = chunks * PIECES * rest, chunks * rest
    shape = (slim, long) if dim else (long, slim)
    row, at = iota(shape, 1 - dim), iota(shape, dim)
    chunk = row >> (rest.bit_length() - 1)
    return one_hot(at == chunk * (PIECES * rest) + piece * rest + (row & (rest - 1)))


def whole_piece(capacity, ref, piece, packed):
    main = capacity // 8 * 8
    rest = capacity - main
    chunks, short = ref.shape[0], ref.shape[2]
    first = ref[:, piece * main : (piece + 1) * main, :].reshape(chunks * main, short)
    last = dot(rest_table(chunks, rest, piece, 1), packed).astype(BF16)
    return first, last


def packed_rest(capacity, ref):
    main = capacity // 8 * 8
    rest = capacity - main
    return ref[:, PIECES * main :, :].reshape(ref.shape[0] * PIECES * rest, ref.shape[2])


def joined(capacity, ref, piece, packed):
    return jnp.concatenate(whole_piece(capacity, ref, piece, packed), axis=0)


def pre_kernel(capacity, rows_ref, w_in_ref, pre_ref):
    short = rows_ref.shape[2]
    packed = packed_rest(capacity, rows_ref)
    total = None
    for p in range(PIECES):
        term = dot(joined(capacity, rows_ref, p, packed), w_in_ref[p * short : (p + 1) * short, :])
        total = term if total is None else total + term
    pre_ref[...] = total


def expert_kernel(capacity, parts, place_ref, rows_hbm, pre_hbm, w_in_hbm, w_out_hbm,
                  back_ref, own_ref, up_ref, down_ref,
                  hold_ref, held_ref, rows_ref, pre_ref, w_in_ref, w_out_ref, sems, in_sems):
    chunks, short = rows_ref.shape[0], rows_ref.shape[2]
    main = capacity // 8 * 8
    rest = capacity - main
    fetch_rows = pltpu.make_async_copy(rows_hbm, rows_ref, in_sems.at[0])
    fetch_rows.start()
    fetches = []
    for p in range(PIECES):
        at = pl.ds(p * short, short)
        fetches.append(pltpu.make_async_copy(w_out_hbm.at[:, at], w_out_ref.at[p], in_sems.at[2 + p]))
        fetches[-1].start()
    fetch_pre = pltpu.make_async_copy(pre_hbm, pre_ref, in_sems.at[1])
    fetch_pre.start()
    for p in range(PIECES):
        at = pl.ds(p * short, short)
        fetches.append(pltpu.make_async_copy(w_in_hbm.at[at, :], w_in_ref.at[p], in_sems.at[2 + PIECES + p]))
        fetches[-1].start()
    fetch_rows.wait()
    packed = packed_rest(capacity, rows_ref)
    total = None
    for p in range(PIECES):
        whole = joined(capacity, rows_ref, p, packed)
        fetches[p].wait()
        term = dot(whole, w_out_ref[p], ((1,), (1,)))
        total = term if total is None else total + term
    fetch_pre.wait()
    grad_pre = (total * silu_grad(pre_ref[...])).astype(BF16)
    hold_ref[...] = grad_pre
    width = own_ref.shape[1]
    me = place_ref[0]
    copies = []
    for i, (ref, step) in enumerate(((up_ref, 1), (down_ref, parts - 1), (own_ref, 0))):
        at = pl.ds(pl.multiple_of(lax.rem(me + step, parts) * width, width), width)
        copies.append(pltpu.make_async_copy(hold_ref.at[:, at], ref, sems.at[i]))
        copies[-1].start()
    last = None
    for p in range(PIECES):
        fetches[PIECES + p].wait()
        piece = dot(grad_pre, w_in_ref[p], ((1,), (1,))).astype(BF16)
        held_ref[:, p * main : (p + 1) * main, :] = piece[: chunks * main].reshape(chunks, main, short)
        at = pl.ds(p * main, main)
        copies.append(pltpu.make_async_copy(held_ref.at[:, at, :], back_ref.at[:, at, :], sems.at[3 + p]))
        copies[-1].start()
        term = dot(rest_table(chunks, rest, p, 0), piece[chunks * main :])
        last = term if last is None else last + term
    held_ref[:, PIECES * main :, :] = last.astype(BF16).reshape(chunks, PIECES * rest, short)
    at = pl.ds(PIECES * main, PIECES * rest)
    copies.append(pltpu.make_async_copy(held_ref.at[:, at, :], back_ref.at[:, at, :], sems.at[3 + PIECES]))
    copies[-1].start()
    for copy in copies:
        copy.wait()


def weight_kernel(capacity, *refs):
    out_ref, done_ref = refs[-2:]
    refs = refs[:-1]
    half = (len(refs) - 1) // 2
    done_ref[...] = jnp.zeros(done_ref.shape, F32)
    chunks, _, short = refs[0].shape
    main = capacity // 8 * 8
    grads = []
    for ref in refs[half:-1]:
        grads += [ref[: chunks * main], ref[chunks * main :]]
    grads = jnp.concatenate(grads, axis=0)
    rests = [packed_rest(capacity, ref) for ref in refs[:half]]
    for p in range(PIECES):
        rows = []
        for ref, packed in zip(refs[:half], rests, strict=True):
            rows += list(whole_piece(capacity, ref, p, packed))
        total = dot(jnp.concatenate(rows, axis=0), grads, ((0,), (0,)))
        out_ref[p * short : (p + 1) * short, :] = total.astype(BF16)


VMEM = pl.BlockSpec(memory_space=pltpu.VMEM)
SMEM = pl.BlockSpec(memory_space=pltpu.SMEM)
ANY = pl.BlockSpec(memory_space=pl.ANY)


def in_hbm(value):
    return pltpu.with_memory_space_constraint(value, pltpu.HBM)


def call(kernel, outs, args, specs=None, out_spec=VMEM, scratch=(), flops=10**9, moved=4 * 10**6):
    many = isinstance(outs, tuple)
    return pl.pallas_call(
        kernel,
        out_shape=outs,
        in_specs=specs or [VMEM] * len(args),
        out_specs=(out_spec,) * len(outs) if many else out_spec,
        scratch_shapes=list(scratch),
        compiler_params=pltpu.CompilerParams(vmem_limit_bytes=24 * 2**20),
        cost_estimate=pl.CostEstimate(flops=flops, bytes_accessed=moved, transcendentals=0),
    )(*args)


def body(saved_b, route_b, gate_b, grad_y_b, w_in, w_out):
    experts = lax.axis_size("expert")
    parts = lax.axis_size("dp")
    tokens, width = saved_b.shape[1:]
    hidden = w_in.shape[3]
    capacity = max(2, tokens * 5 // (4 * experts))
    chunk, short = PIECES * capacity, width // PIECES
    count = experts * chunk
    table = jax.ShapeDtypeStruct((count, short), BF16)
    route, weight_in, weight_out = route_b[0], w_in[0, 0], w_out[0, 0]

    def exchange(rows):
        return lax.all_to_all(rows, "expert", split_axis=0, concat_axis=0, tiled=True)

    arrived = passed_along(grad_y_b, "segment", -1)[0]
    send_x = call(functools.partial(dispatch_x_kernel, capacity, experts), table, (route, saved_b[0]))
    recv_x = exchange(send_x.reshape(experts, chunk, short))
    send_g = call(functools.partial(dispatch_g_kernel, capacity, experts), table, (route, gate_b[0], arrived))
    recv_g = exchange(send_g.reshape(experts, chunk, short))
    x_from_below = passed_along(recv_x, "dp", 1)
    x_from_above = passed_along(recv_x, "dp", -1)
    pre = call(
        functools.partial(pre_kernel, capacity),
        pltpu.HBM((experts * capacity, hidden), F32),
        (recv_x, weight_in),
        flops=1000,
        moved=1000,
    )
    columns = pltpu.HBM((experts * capacity, hidden // parts), BF16)
    me = lax.axis_index("dp").astype(jnp.int32).reshape(1)
    back, own, up, down = call(
        functools.partial(expert_kernel, capacity, parts),
        (pltpu.HBM((experts, chunk, short), BF16), columns, columns, columns),
        (me, in_hbm(recv_g), in_hbm(pre), in_hbm(weight_in), in_hbm(weight_out)),
        specs=[SMEM, ANY, ANY, ANY, ANY],
        out_spec=ANY,
        scratch=[
            pltpu.VMEM((experts * capacity, hidden), BF16),
            pltpu.VMEM((experts, chunk, short), BF16),
            pltpu.VMEM((experts, chunk, short), BF16),
            pltpu.VMEM((experts * capacity, hidden), F32),
            pltpu.VMEM((PIECES, short, hidden), BF16),
            pltpu.VMEM((PIECES, hidden, short), BF16),
            pltpu.SemaphoreType.DMA((4 + PIECES,)),
            pltpu.SemaphoreType.DMA((2 + 2 * PIECES,)),
        ],
        flops=1000,
        moved=1000,
    )
    home = exchange(back)
    g_from_below = passed_along(up, "dp", 1)
    g_from_above = passed_along(down, "dp", -1)
    grad_in, done = call(
        functools.partial(weight_kernel, capacity),
        (jax.ShapeDtypeStruct((width, hidden // parts), BF16), jax.ShapeDtypeStruct((8, 128), F32)),
        (recv_x, x_from_below, x_from_above, own, g_from_below, g_from_above),
        flops=5*10**12,
    )
    grad_x = call(
        functools.partial(combine_kernel, capacity),
        jax.ShapeDtypeStruct((tokens, width), BF16),
        (route, home.reshape(count, short), done),
        flops=1000,
        moved=1000,
    )
    return (grad_x[None], grad_in[None, None])


def solution(mesh):
    return jax.shard_map(
        body,
        mesh=mesh,
        in_specs=(
            P("segment", ("dp", "expert"), None),
            P("segment", ("dp", "expert"), None),
            P("segment", ("dp", "expert"), None),
            P("segment", ("dp", "expert"), None),
            P("segment", "expert", None, None),
            P("segment", "expert", None, None),
        ),
        out_specs=(P("segment", ("dp", "expert"), None), P("segment", "expert", None, "dp")),
        check_vma=False,
    )
```

```python
import functools

import jax
import jax.numpy as jnp
from jax import lax
from jax.experimental import pallas as pl
from jax.experimental.pallas import tpu as pltpu
from jax.sharding import PartitionSpec as P

AXES = ("segment", "dp", "expert")
LOW = 4
PIECES = 4
F32 = jnp.float32
BF16 = jnp.bfloat16


def passed_along(value, axis, steps):
    count = lax.axis_size(axis)
    pairs = [(source, (source + steps) % count) for source in range(count)]
    return lax.ppermute(value, axis, pairs)


def token_groups():
    sections, parts, experts = (lax.axis_size(axis) for axis in AXES)
    line = parts * LOW
    groups = []
    for section in range(sections):
        shift = LOW // 2 if section % 2 else 0
        for part in range(parts):
            where = {}
            for step in range(LOW):
                spot = (part * LOW + shift + step) % line
                for far in range(experts // LOW):
                    expert = far * LOW + spot % LOW
                    where[expert] = (section * parts + spot // LOW) * experts + expert
            groups.append([where[expert] for expert in range(experts)])
    return groups


def silu_grad(value):
    sigma = jax.nn.sigmoid(value)
    return sigma * (1.0 + value * (1.0 - sigma))


def iota(shape, dim):
    return lax.broadcasted_iota(jnp.int32, shape, dim)


def one_hot(condition):
    return jnp.where(condition, 1.0, 0.0).astype(BF16)


def dot(a, b, contract=((1,), (0,))):
    return lax.dot_general(a, b, (contract, ((), ())), preferred_element_type=F32)


def first_short_row(route, rank, capacity, piece):
    main = capacity // 8 * 8
    rest = capacity - main
    inside = jnp.where(rank < main, piece * main + rank, PIECES * main + piece * rest + rank - main)
    return route * (PIECES * capacity) + inside


def slots_along_lanes(route, experts):
    tokens = route.shape[1]
    square = (tokens, tokens)
    lane_route = route.astype(F32)
    named = one_hot(iota((experts, tokens), 0).astype(F32) == lane_route)
    before = dot(named, one_hot(iota(square, 0) < iota(square, 1)))
    rank = jnp.sum(before * named.astype(F32), axis=0, keepdims=True)
    return lane_route.astype(jnp.int32), rank.astype(jnp.int32)


def upright(row):
    square = (row.shape[1], row.shape[1])
    return jnp.sum(
        jnp.where(iota(square, 0) == iota(square, 1), row.astype(F32), 0.0), axis=1, keepdims=True
    )


def slots_along_sublanes(route):
    tokens = route.shape[0]
    square = (tokens, tokens)
    named = one_hot(iota(square, 1) == route)
    before = dot(one_hot(iota(square, 1) < iota(square, 0)), named)
    return jnp.sum(before * named.astype(F32), axis=1, keepdims=True).astype(jnp.int32)


def place(route, values, capacity, experts, rows):
    tokens, width = values.shape
    short = width // PIECES
    lane_route, rank = slots_along_lanes(route, experts)
    at = iota((rows, tokens), 0)
    table = jnp.concatenate(
        [one_hot(at == first_short_row(lane_route, rank, capacity, p)) for p in range(PIECES)], axis=1
    )
    stacked = jnp.concatenate([values[:, p * short : (p + 1) * short] for p in range(PIECES)], axis=0)
    return dot(table, stacked).astype(BF16)


def dispatch_x_kernel(capacity, experts, route_ref, values_ref, out_ref):
    out_ref[...] = place(route_ref[...], values_ref[...], capacity, experts, out_ref.shape[0])


def dispatch_g_kernel(capacity, experts, route_ref, gate_ref, values_ref, out_ref):
    scaled = (upright(gate_ref[...]) * values_ref[...].astype(F32)).astype(BF16)
    out_ref[...] = place(route_ref[...], scaled, capacity, experts, out_ref.shape[0])


def combine_kernel(capacity, route_ref, rows_hbm, _after_ref, out_hbm, rows_ref, out_ref, sem, sems):
    fetch = pltpu.make_async_copy(rows_hbm, rows_ref, sem)
    fetch.start()
    route = upright(route_ref[...]).astype(jnp.int32)
    rank = slots_along_sublanes(route)
    count, short = rows_ref.shape
    at = iota((route.shape[0], count), 1)
    tables = [one_hot(at == first_short_row(route, rank, capacity, p)) for p in range(PIECES)]
    fetch.wait()
    copies = []
    for p, table in enumerate(tables):
        here = pl.ds(p * short, short)
        out_ref[:, p * short : (p + 1) * short] = dot(table, rows_ref[...]).astype(BF16)
        copies.append(pltpu.make_async_copy(out_ref.at[:, here], out_hbm.at[:, here], sems.at[p]))
        copies[-1].start()
    for copy in copies:
        copy.wait()


def rest_table(chunks, rest, piece, dim):
    long, slim = chunks * PIECES * rest, chunks * rest
    shape = (slim, long) if dim else (long, slim)
    row, at = iota(shape, 1 - dim), iota(shape, dim)
    chunk = row >> (rest.bit_length() - 1)
    return one_hot(at == chunk * (PIECES * rest) + piece * rest + (row & (rest - 1)))


def whole_piece(capacity, ref, piece, packed):
    main = capacity // 8 * 8
    rest = capacity - main
    chunks, short = ref.shape[0], ref.shape[2]
    first = ref[:, piece * main : (piece + 1) * main, :].reshape(chunks * main, short)
    last = dot(rest_table(chunks, rest, piece, 1), packed).astype(BF16)
    return first, last


def packed_rest(capacity, ref):
    main = capacity // 8 * 8
    rest = capacity - main
    return ref[:, PIECES * main :, :].reshape(ref.shape[0] * PIECES * rest, ref.shape[2])


def joined(capacity, ref, piece, packed):
    return jnp.concatenate(whole_piece(capacity, ref, piece, packed), axis=0)


def pre_kernel(capacity, rows_ref, w_in_ref, pre_ref):
    short = rows_ref.shape[2]
    packed = packed_rest(capacity, rows_ref)
    total = None
    for p in range(PIECES):
        term = dot(joined(capacity, rows_ref, p, packed), w_in_ref[p * short : (p + 1) * short, :])
        total = term if total is None else total + term
    pre_ref[...] = total


def expert_kernel(capacity, parts, place_ref, rows_hbm, pre_hbm, w_in_hbm, w_out_hbm,
                  back_ref, own_ref, up_ref, down_ref,
                  hold_ref, held_ref, rows_ref, pre_ref, w_in_ref, w_out_ref, sems, in_sems):
    chunks, short = rows_ref.shape[0], rows_ref.shape[2]
    main = capacity // 8 * 8
    rest = capacity - main
    fetch_rows = pltpu.make_async_copy(rows_hbm, rows_ref, in_sems.at[0])
    fetch_rows.start()
    fetches = []
    for p in range(PIECES):
        at = pl.ds(p * short, short)
        fetches.append(pltpu.make_async_copy(w_out_hbm.at[:, at], w_out_ref.at[p], in_sems.at[2 + p]))
        fetches[-1].start()
    fetch_pre = pltpu.make_async_copy(pre_hbm, pre_ref, in_sems.at[1])
    fetch_pre.start()
    for p in range(PIECES):
        at = pl.ds(p * short, short)
        fetches.append(pltpu.make_async_copy(w_in_hbm.at[at, :], w_in_ref.at[p], in_sems.at[2 + PIECES + p]))
        fetches[-1].start()
    fetch_rows.wait()
    packed = packed_rest(capacity, rows_ref)
    total = None
    for p in range(PIECES):
        whole = joined(capacity, rows_ref, p, packed)
        fetches[p].wait()
        term = dot(whole, w_out_ref[p], ((1,), (1,)))
        total = term if total is None else total + term
    fetch_pre.wait()
    grad_pre = (total * silu_grad(pre_ref[...])).astype(BF16)
    hold_ref[...] = grad_pre
    width = own_ref.shape[1]
    me = place_ref[0]
    copies = []
    for i, (ref, step) in enumerate(((up_ref, 1), (down_ref, parts - 1), (own_ref, 0))):
        at = pl.ds(pl.multiple_of(lax.rem(me + step, parts) * width, width), width)
        copies.append(pltpu.make_async_copy(hold_ref.at[:, at], ref, sems.at[i]))
        copies[-1].start()
    last = None
    for p in range(PIECES):
        fetches[PIECES + p].wait()
        piece = dot(grad_pre, w_in_ref[p], ((1,), (1,))).astype(BF16)
        held_ref[:, p * main : (p + 1) * main, :] = piece[: chunks * main].reshape(chunks, main, short)
        at = pl.ds(p * main, main)
        copies.append(pltpu.make_async_copy(held_ref.at[:, at, :], back_ref.at[:, at, :], sems.at[3 + p]))
        copies[-1].start()
        term = dot(rest_table(chunks, rest, p, 0), piece[chunks * main :])
        last = term if last is None else last + term
    held_ref[:, PIECES * main :, :] = last.astype(BF16).reshape(chunks, PIECES * rest, short)
    at = pl.ds(PIECES * main, PIECES * rest)
    copies.append(pltpu.make_async_copy(held_ref.at[:, at, :], back_ref.at[:, at, :], sems.at[3 + PIECES]))
    copies[-1].start()
    for copy in copies:
        copy.wait()


def weight_kernel(capacity, *refs):
    out_ref, done_ref = refs[-2:]
    refs = refs[:-1]
    half = (len(refs) - 1) // 2
    done_ref[...] = jnp.zeros(done_ref.shape, F32)
    chunks, _, short = refs[0].shape
    main = capacity // 8 * 8
    grads = []
    for ref in refs[half:-1]:
        grads += [ref[: chunks * main], ref[chunks * main :]]
    grads = jnp.concatenate(grads, axis=0)
    rests = [packed_rest(capacity, ref) for ref in refs[:half]]
    for p in range(PIECES):
        rows = []
        for ref, packed in zip(refs[:half], rests, strict=True):
            rows += list(whole_piece(capacity, ref, p, packed))
        total = dot(jnp.concatenate(rows, axis=0), grads, ((0,), (0,)))
        out_ref[p * short : (p + 1) * short, :] = total.astype(BF16)


VMEM = pl.BlockSpec(memory_space=pltpu.VMEM)
SMEM = pl.BlockSpec(memory_space=pltpu.SMEM)
ANY = pl.BlockSpec(memory_space=pl.ANY)


def in_hbm(value):
    return pltpu.with_memory_space_constraint(value, pltpu.HBM)


def call(kernel, outs, args, specs=None, out_spec=VMEM, scratch=(), flops=10**9, moved=4 * 10**6):
    many = isinstance(outs, tuple)
    return pl.pallas_call(
        kernel,
        out_shape=outs,
        in_specs=specs or [VMEM] * len(args),
        out_specs=(out_spec,) * len(outs) if many else out_spec,
        scratch_shapes=list(scratch),
        compiler_params=pltpu.CompilerParams(vmem_limit_bytes=24 * 2**20),
        name=getattr(kernel, "func", kernel).__name__.split("_")[0],
        cost_estimate=pl.CostEstimate(flops=flops, bytes_accessed=moved, transcendentals=0),
    )(*args)


def body(saved_b, route_b, gate_b, grad_y_b, w_in, w_out):
    experts = lax.axis_size("expert")
    parts = lax.axis_size("dp")
    tokens, width = saved_b.shape[1:]
    hidden = w_in.shape[3]
    capacity = max(2, tokens * 5 // (4 * experts))
    chunk, short = PIECES * capacity, width // PIECES
    count = experts * chunk
    table = jax.ShapeDtypeStruct((count, short), BF16)
    route, gate = route_b.reshape(1, tokens), gate_b.reshape(1, tokens)
    weight_in, weight_out = w_in[0, 0], w_out[0, 0]

    def exchange(rows):
        return lax.all_to_all(
            rows, AXES, split_axis=0, concat_axis=0, tiled=True, axis_index_groups=token_groups()
        )

    arrived = passed_along(grad_y_b, "segment", -1)[0]
    send_x = call(functools.partial(dispatch_x_kernel, capacity, experts), table, (route, saved_b[0]))
    recv_x = exchange(send_x.reshape(experts, chunk, short))
    send_g = call(functools.partial(dispatch_g_kernel, capacity, experts), table, (route, gate, arrived))
    recv_g = exchange(send_g.reshape(experts, chunk, short))
    x_from_below = passed_along(recv_x, "dp", 1)
    x_from_above = passed_along(recv_x, "dp", -1)
    pre = call(
        functools.partial(pre_kernel, capacity),
        pltpu.HBM((experts * capacity, hidden), F32),
        (recv_x, weight_in),
        flops=2*10**13,
        moved=1000,
    )
    columns = pltpu.HBM((experts * capacity, hidden // parts), BF16)
    me = lax.axis_index("dp").astype(jnp.int32).reshape(1)
    back, own, up, down = call(
        functools.partial(expert_kernel, capacity, parts),
        (pltpu.HBM((experts, chunk, short), BF16), columns, columns, columns),
        (me, in_hbm(recv_g), in_hbm(pre), in_hbm(weight_in), in_hbm(weight_out)),
        specs=[SMEM, ANY, ANY, ANY, ANY],
        out_spec=ANY,
        scratch=[
            pltpu.VMEM((experts * capacity, hidden), BF16),
            pltpu.VMEM((experts, chunk, short), BF16),
            pltpu.VMEM((experts, chunk, short), BF16),
            pltpu.VMEM((experts * capacity, hidden), F32),
            pltpu.VMEM((PIECES, short, hidden), BF16),
            pltpu.VMEM((PIECES, hidden, short), BF16),
            pltpu.SemaphoreType.DMA((4 + PIECES,)),
            pltpu.SemaphoreType.DMA((2 + 2 * PIECES,)),
        ],
        flops=5*10**12,
        moved=1000,
    )
    home = exchange(back)
    g_from_below = passed_along(up, "dp", 1)
    g_from_above = passed_along(down, "dp", -1)
    grad_in, done = call(
        functools.partial(weight_kernel, capacity),
        (jax.ShapeDtypeStruct((width, hidden // parts), BF16), jax.ShapeDtypeStruct((8, 128), F32)),
        (recv_x, x_from_below, x_from_above, own, g_from_below, g_from_above),
        flops=5*10**12,
    )
    grad_x = call(
        functools.partial(combine_kernel, capacity),
        pltpu.HBM((tokens, width), BF16),
        (route, in_hbm(home.reshape(count, short)), done),
        specs=[VMEM, ANY, VMEM],
        out_spec=ANY,
        scratch=[
            pltpu.VMEM((count, short), BF16),
            pltpu.VMEM((tokens, width), BF16),
            pltpu.SemaphoreType.DMA(()),
            pltpu.SemaphoreType.DMA((PIECES,)),
        ],
        flops=1000,
        moved=1000,
    )
    return (grad_x[None], grad_in[None, None])


def solution(mesh):
    return jax.shard_map(
        body,
        mesh=mesh,
        in_specs=(
            P("segment", ("dp", "expert"), None),
            P("segment", ("dp", "expert"), None),
            P("segment", ("dp", "expert"), None),
            P("segment", ("dp", "expert"), None),
            P("segment", "expert", None, None),
            P("segment", "expert", None, None),
        ),
        out_specs=(P("segment", ("dp", "expert"), None), P("segment", "expert", None, "dp")),
        check_vma=False,
    )
```

```python
import functools

import jax
import jax.numpy as jnp
from jax import lax
from jax.experimental import pallas as pl
from jax.experimental.pallas import tpu as pltpu
from jax.sharding import PartitionSpec as P

AXES = ("segment", "dp", "expert")
LOW = 4
PIECES = 4
F32 = jnp.float32
BF16 = jnp.bfloat16


def passed_along(value, axis, steps):
    count = lax.axis_size(axis)
    pairs = [(source, (source + steps) % count) for source in range(count)]
    return lax.ppermute(value, axis, pairs)


def token_groups():
    sections, parts, experts = (lax.axis_size(axis) for axis in AXES)
    line = parts * LOW
    groups = []
    for section in range(sections):
        shift = LOW // 2 if section % 2 else 0
        for part in range(parts):
            where = {}
            for step in range(LOW):
                spot = (part * LOW + shift + step) % line
                for far in range(experts // LOW):
                    expert = far * LOW + spot % LOW
                    where[expert] = (section * parts + spot // LOW) * experts + expert
            groups.append([where[expert] for expert in range(experts)])
    return groups


def silu_grad(value):
    sigma = jax.nn.sigmoid(value)
    return sigma * (1.0 + value * (1.0 - sigma))


def iota(shape, dim):
    return lax.broadcasted_iota(jnp.int32, shape, dim)


def one_hot(condition):
    return jnp.where(condition, 1.0, 0.0).astype(BF16)


def dot(a, b, contract=((1,), (0,))):
    return lax.dot_general(a, b, (contract, ((), ())), preferred_element_type=F32)


def first_short_row(route, rank, capacity, piece):
    main = capacity // 8 * 8
    rest = capacity - main
    inside = jnp.where(rank < main, piece * main + rank, PIECES * main + piece * rest + rank - main)
    return route * (PIECES * capacity) + inside


def slots_along_lanes(route, experts):
    tokens = route.shape[1]
    square = (tokens, tokens)
    lane_route = route.astype(F32)
    named = one_hot(iota((experts, tokens), 0).astype(F32) == lane_route)
    before = dot(named, one_hot(iota(square, 0) < iota(square, 1)))
    rank = jnp.sum(before * named.astype(F32), axis=0, keepdims=True)
    return lane_route.astype(jnp.int32), rank.astype(jnp.int32)


def upright(row):
    square = (row.shape[1], row.shape[1])
    return jnp.sum(
        jnp.where(iota(square, 0) == iota(square, 1), row.astype(F32), 0.0), axis=1, keepdims=True
    )


def slots_along_sublanes(route):
    tokens = route.shape[0]
    square = (tokens, tokens)
    named = one_hot(iota(square, 1) == route)
    before = dot(one_hot(iota(square, 1) < iota(square, 0)), named)
    return jnp.sum(before * named.astype(F32), axis=1, keepdims=True).astype(jnp.int32)


def dispatch_kernel(capacity, experts, refs, scale):
    route_hbm, values_hbm, out_hbm, route_ref, values_ref, out_ref, sems = refs
    fetch_route = pltpu.make_async_copy(route_hbm, route_ref, sems.at[0])
    fetch_route.start()
    fetch_values = pltpu.make_async_copy(values_hbm, values_ref, sems.at[1])
    fetch_values.start()
    fetch_route.wait()
    rows = out_ref.shape[0]
    tokens, width = values_ref.shape
    short = width // PIECES
    lane_route, rank = slots_along_lanes(route_ref[...], experts)
    at = iota((rows, tokens), 0)
    table = jnp.concatenate(
        [one_hot(at == first_short_row(lane_route, rank, capacity, p)) for p in range(PIECES)], axis=1
    )
    fetch_values.wait()
    values = scale(values_ref[...])
    stacked = jnp.concatenate([values[:, p * short : (p + 1) * short] for p in range(PIECES)], axis=0)
    copies = []
    half = rows // 2
    for i in range(2):
        here = pl.ds(i * half, half)
        out_ref[here, :] = dot(table[i * half : (i + 1) * half], stacked).astype(BF16)
        copies.append(pltpu.make_async_copy(out_ref.at[here, :], out_hbm.at[here, :], sems.at[2 + i]))
        copies[-1].start()
    for copy in copies:
        copy.wait()


def dispatch_x_kernel(capacity, experts, *refs):
    dispatch_kernel(capacity, experts, refs, lambda values: values)


def dispatch_g_kernel(capacity, experts, gate_ref, *refs):
    gate = upright(gate_ref[...])
    dispatch_kernel(capacity, experts, refs, lambda values: (gate * values.astype(F32)).astype(BF16))


def combine_kernel(capacity, route_ref, rows_hbm, _after_ref, out_hbm, rows_ref, out_ref, sem, sems):
    fetch = pltpu.make_async_copy(rows_hbm, rows_ref, sem)
    fetch.start()
    route = upright(route_ref[...]).astype(jnp.int32)
    rank = slots_along_sublanes(route)
    count, short = rows_ref.shape
    at = iota((route.shape[0], count), 1)
    tables = [one_hot(at == first_short_row(route, rank, capacity, p)) for p in range(PIECES)]
    fetch.wait()
    copies = []
    for p, table in enumerate(tables):
        here = pl.ds(p * short, short)
        out_ref[:, p * short : (p + 1) * short] = dot(table, rows_ref[...]).astype(BF16)
        copies.append(pltpu.make_async_copy(out_ref.at[:, here], out_hbm.at[:, here], sems.at[p]))
        copies[-1].start()
    for copy in copies:
        copy.wait()


def rest_table(chunks, rest, piece, dim):
    long, slim = chunks * PIECES * rest, chunks * rest
    shape = (slim, long) if dim else (long, slim)
    row, at = iota(shape, 1 - dim), iota(shape, dim)
    chunk = row >> (rest.bit_length() - 1)
    return one_hot(at == chunk * (PIECES * rest) + piece * rest + (row & (rest - 1)))


def whole_piece(capacity, ref, piece, packed):
    main = capacity // 8 * 8
    rest = capacity - main
    chunks, short = ref.shape[0], ref.shape[2]
    first = ref[:, piece * main : (piece + 1) * main, :].reshape(chunks * main, short)
    last = dot(rest_table(chunks, rest, piece, 1), packed).astype(BF16)
    return first, last


def packed_rest(capacity, ref):
    main = capacity // 8 * 8
    rest = capacity - main
    return ref[:, PIECES * main :, :].reshape(ref.shape[0] * PIECES * rest, ref.shape[2])


def joined(capacity, ref, piece, packed):
    return jnp.concatenate(whole_piece(capacity, ref, piece, packed), axis=0)


def pre_kernel(capacity, rows_ref, w_in_ref, pre_ref):
    short = rows_ref.shape[2]
    packed = packed_rest(capacity, rows_ref)
    total = None
    for p in range(PIECES):
        term = dot(joined(capacity, rows_ref, p, packed), w_in_ref[p * short : (p + 1) * short, :])
        total = term if total is None else total + term
    pre_ref[...] = total


def expert_kernel(capacity, parts, place_ref, rows_hbm, pre_hbm, w_in_hbm, w_out_hbm,
                  back_ref, own_ref, up_ref, down_ref,
                  hold_ref, held_ref, rows_ref, pre_ref, w_in_ref, w_out_ref, sems, in_sems):
    chunks, short = rows_ref.shape[0], rows_ref.shape[2]
    main = capacity // 8 * 8
    rest = capacity - main
    fetch_rows = pltpu.make_async_copy(rows_hbm, rows_ref, in_sems.at[0])
    fetch_rows.start()
    fetches = []
    for p in range(PIECES):
        at = pl.ds(p * short, short)
        fetches.append(pltpu.make_async_copy(w_out_hbm.at[:, at], w_out_ref.at[p], in_sems.at[2 + p]))
        fetches[-1].start()
    fetch_pre = pltpu.make_async_copy(pre_hbm, pre_ref, in_sems.at[1])
    fetch_pre.start()
    for p in range(PIECES):
        at = pl.ds(p * short, short)
        fetches.append(pltpu.make_async_copy(w_in_hbm.at[at, :], w_in_ref.at[p], in_sems.at[2 + PIECES + p]))
        fetches[-1].start()
    fetch_rows.wait()
    packed = packed_rest(capacity, rows_ref)
    total = None
    for p in range(PIECES):
        whole = joined(capacity, rows_ref, p, packed)
        fetches[p].wait()
        term = dot(whole, w_out_ref[p], ((1,), (1,)))
        total = term if total is None else total + term
    fetch_pre.wait()
    grad_pre = (total * silu_grad(pre_ref[...])).astype(BF16)
    hold_ref[...] = grad_pre
    width = own_ref.shape[1]
    me = place_ref[0]
    copies = []
    for i, (ref, step) in enumerate(((up_ref, 1), (down_ref, parts - 1), (own_ref, 0))):
        at = pl.ds(pl.multiple_of(lax.rem(me + step, parts) * width, width), width)
        copies.append(pltpu.make_async_copy(hold_ref.at[:, at], ref, sems.at[i]))
        copies[-1].start()
    last = None
    for p in range(PIECES):
        fetches[PIECES + p].wait()
        piece = dot(grad_pre, w_in_ref[p], ((1,), (1,))).astype(BF16)
        held_ref[:, p * main : (p + 1) * main, :] = piece[: chunks * main].reshape(chunks, main, short)
        at = pl.ds(p * main, main)
        copies.append(pltpu.make_async_copy(held_ref.at[:, at, :], back_ref.at[:, at, :], sems.at[3 + p]))
        copies[-1].start()
        term = dot(rest_table(chunks, rest, p, 0), piece[chunks * main :])
        last = term if last is None else last + term
    held_ref[:, PIECES * main :, :] = last.astype(BF16).reshape(chunks, PIECES * rest, short)
    at = pl.ds(PIECES * main, PIECES * rest)
    copies.append(pltpu.make_async_copy(held_ref.at[:, at, :], back_ref.at[:, at, :], sems.at[3 + PIECES]))
    copies[-1].start()
    for copy in copies:
        copy.wait()


def weight_kernel(capacity, *refs):
    out_ref, done_ref = refs[-2:]
    refs = refs[:-1]
    half = (len(refs) - 1) // 2
    done_ref[...] = jnp.zeros(done_ref.shape, F32)
    chunks, _, short = refs[0].shape
    main = capacity // 8 * 8
    grads = []
    for ref in refs[half:-1]:
        grads += [ref[: chunks * main], ref[chunks * main :]]
    grads = jnp.concatenate(grads, axis=0)
    rests = [packed_rest(capacity, ref) for ref in refs[:half]]
    for p in range(PIECES):
        rows = []
        for ref, packed in zip(refs[:half], rests, strict=True):
            rows += list(whole_piece(capacity, ref, p, packed))
        total = dot(jnp.concatenate(rows, axis=0), grads, ((0,), (0,)))
        out_ref[p * short : (p + 1) * short, :] = total.astype(BF16)


VMEM = pl.BlockSpec(memory_space=pltpu.VMEM)
SMEM = pl.BlockSpec(memory_space=pltpu.SMEM)
ANY = pl.BlockSpec(memory_space=pl.ANY)


def in_hbm(value):
    return pltpu.with_memory_space_constraint(value, pltpu.HBM)


def call(kernel, outs, args, specs=None, out_spec=VMEM, scratch=(), flops=10**9, moved=4 * 10**6):
    many = isinstance(outs, tuple)
    return pl.pallas_call(
        kernel,
        out_shape=outs,
        in_specs=specs or [VMEM] * len(args),
        out_specs=(out_spec,) * len(outs) if many else out_spec,
        scratch_shapes=list(scratch),
        compiler_params=pltpu.CompilerParams(vmem_limit_bytes=24 * 2**20),
        name=getattr(kernel, "func", kernel).__name__.split("_")[0],
        cost_estimate=pl.CostEstimate(flops=flops, bytes_accessed=moved, transcendentals=0),
    )(*args)


def body(saved_b, route_b, gate_b, grad_y_b, w_in, w_out):
    experts = lax.axis_size("expert")
    parts = lax.axis_size("dp")
    tokens, width = saved_b.shape[1:]
    hidden = w_in.shape[3]
    capacity = max(2, tokens * 5 // (4 * experts))
    chunk, short = PIECES * capacity, width // PIECES
    count = experts * chunk
    table = pltpu.HBM((count, short), BF16)
    route, gate = route_b.reshape(1, tokens), gate_b.reshape(1, tokens)
    weight_in, weight_out = w_in[0, 0], w_out[0, 0]

    def exchange(rows):
        return lax.all_to_all(
            rows, AXES, split_axis=0, concat_axis=0, tiled=True, axis_index_groups=token_groups()
        )

    arrived = passed_along(grad_y_b, "segment", -1)[0]
    scratch = [
        pltpu.VMEM((1, tokens), jnp.int32),
        pltpu.VMEM((tokens, width), BF16),
        pltpu.VMEM((count, short), BF16),
        pltpu.SemaphoreType.DMA((4,)),
    ]
    send_x = call(
        functools.partial(dispatch_x_kernel, capacity, experts),
        table,
        (in_hbm(route), in_hbm(saved_b[0])),
        specs=[ANY, ANY],
        out_spec=ANY,
        scratch=scratch,
    )
    recv_x = exchange(send_x.reshape(experts, chunk, short))
    send_g = call(
        functools.partial(dispatch_g_kernel, capacity, experts),
        table,
        (gate, in_hbm(route), in_hbm(arrived)),
        specs=[VMEM, ANY, ANY],
        out_spec=ANY,
        scratch=scratch,
        flops=10**9,
    )
    recv_g = exchange(send_g.reshape(experts, chunk, short))
    x_from_below = passed_along(recv_x, "dp", 1)
    x_from_above = passed_along(recv_x, "dp", -1)
    pre = call(
        functools.partial(pre_kernel, capacity),
        pltpu.HBM((experts * capacity, hidden), F32),
        (recv_x, weight_in),
        flops=2*10**13,
        moved=1000,
    )
    columns = pltpu.HBM((experts * capacity, hidden // parts), BF16)
    me = lax.axis_index("dp").astype(jnp.int32).reshape(1)
    back, own, up, down = call(
        functools.partial(expert_kernel, capacity, parts),
        (pltpu.HBM((experts, chunk, short), BF16), columns, columns, columns),
        (me, in_hbm(recv_g), in_hbm(pre), in_hbm(weight_in), in_hbm(weight_out)),
        specs=[SMEM, ANY, ANY, ANY, ANY],
        out_spec=ANY,
        scratch=[
            pltpu.VMEM((experts * capacity, hidden), BF16),
            pltpu.VMEM((experts, chunk, short), BF16),
            pltpu.VMEM((experts, chunk, short), BF16),
            pltpu.VMEM((experts * capacity, hidden), F32),
            pltpu.VMEM((PIECES, short, hidden), BF16),
            pltpu.VMEM((PIECES, hidden, short), BF16),
            pltpu.SemaphoreType.DMA((4 + PIECES,)),
            pltpu.SemaphoreType.DMA((2 + 2 * PIECES,)),
        ],
        flops=5*10**12,
        moved=1000,
    )
    home = exchange(back)
    g_from_below = passed_along(up, "dp", 1)
    g_from_above = passed_along(down, "dp", -1)
    grad_in, done = call(
        functools.partial(weight_kernel, capacity),
        (jax.ShapeDtypeStruct((width, hidden // parts), BF16), jax.ShapeDtypeStruct((8, 128), F32)),
        (recv_x, x_from_below, x_from_above, own, g_from_below, g_from_above),
        flops=5*10**12,
    )
    grad_x = call(
        functools.partial(combine_kernel, capacity),
        pltpu.HBM((tokens, width), BF16),
        (route, in_hbm(home.reshape(count, short)), done),
        specs=[VMEM, ANY, VMEM],
        out_spec=ANY,
        scratch=[
            pltpu.VMEM((count, short), BF16),
            pltpu.VMEM((tokens, width), BF16),
            pltpu.SemaphoreType.DMA(()),
            pltpu.SemaphoreType.DMA((PIECES,)),
        ],
        flops=1000,
        moved=1000,
    )
    return (grad_x[None], grad_in[None, None])


def solution(mesh):
    return jax.shard_map(
        body,
        mesh=mesh,
        in_specs=(
            P("segment", ("dp", "expert"), None),
            P("segment", ("dp", "expert"), None),
            P("segment", ("dp", "expert"), None),
            P("segment", ("dp", "expert"), None),
            P("segment", "expert", None, None),
            P("segment", "expert", None, None),
        ),
        out_specs=(P("segment", ("dp", "expert"), None), P("segment", "expert", None, "dp")),
        check_vma=False,
    )
```

```python
import functools

import jax
import jax.numpy as jnp
from jax import lax
from jax.experimental import pallas as pl
from jax.experimental.pallas import tpu as pltpu
from jax.sharding import PartitionSpec as P

AXES = ("segment", "dp", "expert")
LOW = 4
PIECES = 4
F32 = jnp.float32
BF16 = jnp.bfloat16


def passed_along(value, axis, steps):
    count = lax.axis_size(axis)
    pairs = [(source, (source + steps) % count) for source in range(count)]
    return lax.ppermute(value, axis, pairs)


def token_groups():
    sections, parts, experts = (lax.axis_size(axis) for axis in AXES)
    line = parts * LOW
    groups = []
    for section in range(sections):
        shift = LOW // 2 if section % 2 else 0
        for part in range(parts):
            where = {}
            for step in range(LOW):
                spot = (part * LOW + shift + step) % line
                for far in range(experts // LOW):
                    expert = far * LOW + spot % LOW
                    where[expert] = (section * parts + spot // LOW) * experts + expert
            groups.append([where[expert] for expert in range(experts)])
    return groups


def silu_grad(value):
    sigma = jax.nn.sigmoid(value)
    return sigma * (1.0 + value * (1.0 - sigma))


def iota(shape, dim):
    return lax.broadcasted_iota(jnp.int32, shape, dim)


def one_hot(condition):
    return jnp.where(condition, 1.0, 0.0).astype(BF16)


def dot(a, b, contract=((1,), (0,))):
    return lax.dot_general(a, b, (contract, ((), ())), preferred_element_type=F32)


def first_short_row(route, rank, capacity, piece):
    main = capacity // 8 * 8
    rest = capacity - main
    inside = jnp.where(rank < main, piece * main + rank, PIECES * main + piece * rest + rank - main)
    return route * (PIECES * capacity) + inside


def slots_along_lanes(route, experts):
    tokens = route.shape[1]
    square = (tokens, tokens)
    lane_route = route.astype(F32)
    named = one_hot(iota((experts, tokens), 0).astype(F32) == lane_route)
    before = dot(named, one_hot(iota(square, 0) < iota(square, 1)))
    rank = jnp.sum(before * named.astype(F32), axis=0, keepdims=True)
    return lane_route.astype(jnp.int32), rank.astype(jnp.int32)


def upright(row):
    square = (row.shape[1], row.shape[1])
    return jnp.sum(
        jnp.where(iota(square, 0) == iota(square, 1), row.astype(F32), 0.0), axis=1, keepdims=True
    )


def slots_along_sublanes(route):
    tokens = route.shape[0]
    square = (tokens, tokens)
    named = one_hot(iota(square, 1) == route)
    before = dot(one_hot(iota(square, 1) < iota(square, 0)), named)
    return jnp.sum(before * named.astype(F32), axis=1, keepdims=True).astype(jnp.int32)


def dispatch_kernel(capacity, experts, refs, scale):
    route_hbm, values_hbm, out_hbm, route_ref, values_ref, out_ref, sems = refs
    fetch_route = pltpu.make_async_copy(route_hbm, route_ref, sems.at[0])
    fetch_route.start()
    fetch_values = pltpu.make_async_copy(values_hbm, values_ref, sems.at[1])
    fetch_values.start()
    fetch_route.wait()
    rows = out_ref.shape[0]
    tokens, width = values_ref.shape
    short = width // PIECES
    lane_route, rank = slots_along_lanes(route_ref[...], experts)
    at = iota((rows, tokens), 0)
    table = jnp.concatenate(
        [one_hot(at == first_short_row(lane_route, rank, capacity, p)) for p in range(PIECES)], axis=1
    )
    fetch_values.wait()
    values = scale(values_ref[...])
    stacked = jnp.concatenate([values[:, p * short : (p + 1) * short] for p in range(PIECES)], axis=0)
    copies = []
    half = rows // 2
    for i in range(2):
        here = pl.ds(i * half, half)
        out_ref[here, :] = dot(table[i * half : (i + 1) * half], stacked).astype(BF16)
        copies.append(pltpu.make_async_copy(out_ref.at[here, :], out_hbm.at[here, :], sems.at[2 + i]))
        copies[-1].start()
    for copy in copies:
        copy.wait()


def dispatch_x_kernel(capacity, experts, *refs):
    dispatch_kernel(capacity, experts, refs, lambda values: values)


def dispatch_g_kernel(capacity, experts, gate_ref, *refs):
    gate = upright(gate_ref[...])
    dispatch_kernel(capacity, experts, refs, lambda values: (gate * values.astype(F32)).astype(BF16))


def combine_kernel(capacity, route_ref, rows_hbm, _after_ref, out_hbm, rows_ref, out_ref, sem, sems):
    fetch = pltpu.make_async_copy(rows_hbm, rows_ref, sem)
    fetch.start()
    route = upright(route_ref[...]).astype(jnp.int32)
    rank = slots_along_sublanes(route)
    count, short = rows_ref.shape
    at = iota((route.shape[0], count), 1)
    tables = [one_hot(at == first_short_row(route, rank, capacity, p)) for p in range(PIECES)]
    fetch.wait()
    copies = []
    for p, table in enumerate(tables):
        here = pl.ds(p * short, short)
        out_ref[:, p * short : (p + 1) * short] = dot(table, rows_ref[...]).astype(BF16)
        copies.append(pltpu.make_async_copy(out_ref.at[:, here], out_hbm.at[:, here], sems.at[p]))
        copies[-1].start()
    for copy in copies:
        copy.wait()


def rest_table(chunks, rest, piece, dim):
    long, slim = chunks * PIECES * rest, chunks * rest
    shape = (slim, long) if dim else (long, slim)
    row, at = iota(shape, 1 - dim), iota(shape, dim)
    chunk = row >> (rest.bit_length() - 1)
    return one_hot(at == chunk * (PIECES * rest) + piece * rest + (row & (rest - 1)))


def whole_piece(capacity, ref, piece, packed):
    main = capacity // 8 * 8
    rest = capacity - main
    chunks, short = ref.shape[0], ref.shape[2]
    first = ref[:, piece * main : (piece + 1) * main, :].reshape(chunks * main, short)
    last = dot(rest_table(chunks, rest, piece, 1), packed).astype(BF16)
    return first, last


def packed_rest(capacity, ref):
    main = capacity // 8 * 8
    rest = capacity - main
    return ref[:, PIECES * main :, :].reshape(ref.shape[0] * PIECES * rest, ref.shape[2])


def joined(capacity, ref, piece, packed):
    return jnp.concatenate(whole_piece(capacity, ref, piece, packed), axis=0)


def pre_kernel(capacity, rows_ref, w_in_ref, pre_ref):
    short = rows_ref.shape[2]
    packed = packed_rest(capacity, rows_ref)
    total = None
    for p in range(PIECES):
        term = dot(joined(capacity, rows_ref, p, packed), w_in_ref[p * short : (p + 1) * short, :])
        total = term if total is None else total + term
    pre_ref[...] = total


def halves_kernel(rows_ref, first_hbm, last_hbm, sems):
    half = first_hbm.shape[0]
    copies = [
        pltpu.make_async_copy(rows_ref.at[i * half : (i + 1) * half], out, sems.at[i])
        for i, out in enumerate((first_hbm, last_hbm))
    ]
    for copy in copies:
        copy.start()
    for copy in copies:
        copy.wait()


def expert_kernel(capacity, parts, place_ref, rows_hbm, pre_hbm, w_in_hbm, w_out_hbm,
                  back_ref, own_ref, up_ref, down_ref,
                  hold_ref, held_ref, rows_ref, pre_ref, w_in_ref, w_out_ref, sems, in_sems):
    chunks, short = rows_ref.shape[0], rows_ref.shape[2]
    main = capacity // 8 * 8
    rest = capacity - main
    fetch_rows = pltpu.make_async_copy(rows_hbm, rows_ref, in_sems.at[0])
    fetch_rows.start()
    fetches = []
    for p in range(PIECES):
        at = pl.ds(p * short, short)
        fetches.append(pltpu.make_async_copy(w_out_hbm.at[:, at], w_out_ref.at[p], in_sems.at[2 + p]))
        fetches[-1].start()
    fetch_pre = pltpu.make_async_copy(pre_hbm, pre_ref, in_sems.at[1])
    fetch_pre.start()
    for p in range(PIECES):
        at = pl.ds(p * short, short)
        fetches.append(pltpu.make_async_copy(w_in_hbm.at[at, :], w_in_ref.at[p], in_sems.at[2 + PIECES + p]))
        fetches[-1].start()
    fetch_rows.wait()
    packed = packed_rest(capacity, rows_ref)
    total = None
    for p in range(PIECES):
        whole = joined(capacity, rows_ref, p, packed)
        fetches[p].wait()
        term = dot(whole, w_out_ref[p], ((1,), (1,)))
        total = term if total is None else total + term
    fetch_pre.wait()
    grad_pre = (total * silu_grad(pre_ref[...])).astype(BF16)
    hold_ref[...] = grad_pre
    width = own_ref.shape[1]
    me = place_ref[0]
    copies = []
    for i, (ref, step) in enumerate(((up_ref, 1), (down_ref, parts - 1), (own_ref, 0))):
        at = pl.ds(pl.multiple_of(lax.rem(me + step, parts) * width, width), width)
        copies.append(pltpu.make_async_copy(hold_ref.at[:, at], ref, sems.at[i]))
        copies[-1].start()
    last = None
    for p in range(PIECES):
        fetches[PIECES + p].wait()
        piece = dot(grad_pre, w_in_ref[p], ((1,), (1,))).astype(BF16)
        held_ref[:, p * main : (p + 1) * main, :] = piece[: chunks * main].reshape(chunks, main, short)
        at = pl.ds(p * main, main)
        copies.append(pltpu.make_async_copy(held_ref.at[:, at, :], back_ref.at[:, at, :], sems.at[3 + p]))
        copies[-1].start()
        term = dot(rest_table(chunks, rest, p, 0), piece[chunks * main :])
        last = term if last is None else last + term
    held_ref[:, PIECES * main :, :] = last.astype(BF16).reshape(chunks, PIECES * rest, short)
    at = pl.ds(PIECES * main, PIECES * rest)
    copies.append(pltpu.make_async_copy(held_ref.at[:, at, :], back_ref.at[:, at, :], sems.at[3 + PIECES]))
    copies[-1].start()
    for copy in copies:
        copy.wait()


def weight_kernel(capacity, own_x_ref, *refs):
    out_ref, done_ref = refs[-2:]
    x_refs, grad_refs = refs[:-5], refs[-5:-2]
    done_ref[...] = jnp.zeros(done_ref.shape, F32)
    chunks, _, short = own_x_ref.shape
    main = capacity // 8 * 8
    rest = capacity - main
    grads = [grad_refs[0][...]]
    for ref in grad_refs[1:]:
        for i in range(2):
            at, then = i * chunks * main // 2, chunks * main + i * chunks * rest // 2
            grads += [ref[at : at + chunks * main // 2], ref[then : then + chunks * rest // 2]]
    grads = jnp.concatenate(grads, axis=0)
    x_refs = (own_x_ref, *x_refs)
    rests = [packed_rest(capacity, ref) for ref in x_refs]
    for p in range(PIECES):
        rows = []
        for ref, packed in zip(x_refs, rests, strict=True):
            rows += list(whole_piece(capacity, ref, p, packed))
        total = dot(jnp.concatenate(rows, axis=0), grads, ((0,), (0,)))
        out_ref[p * short : (p + 1) * short, :] = total.astype(BF16)


VMEM = pl.BlockSpec(memory_space=pltpu.VMEM)
SMEM = pl.BlockSpec(memory_space=pltpu.SMEM)
ANY = pl.BlockSpec(memory_space=pl.ANY)


def in_hbm(value):
    return pltpu.with_memory_space_constraint(value, pltpu.HBM)


def call(kernel, outs, args, specs=None, out_spec=VMEM, scratch=(), flops=10**9, moved=4 * 10**6):
    many = isinstance(outs, tuple)
    return pl.pallas_call(
        kernel,
        out_shape=outs,
        in_specs=specs or [VMEM] * len(args),
        out_specs=(out_spec,) * len(outs) if many else out_spec,
        scratch_shapes=list(scratch),
        compiler_params=pltpu.CompilerParams(vmem_limit_bytes=24 * 2**20),
        name=getattr(kernel, "func", kernel).__name__.split("_")[0],
        cost_estimate=pl.CostEstimate(flops=flops, bytes_accessed=moved, transcendentals=0),
    )(*args)


def body(saved_b, route_b, gate_b, grad_y_b, w_in, w_out):
    experts = lax.axis_size("expert")
    parts = lax.axis_size("dp")
    tokens, width = saved_b.shape[1:]
    hidden = w_in.shape[3]
    capacity = max(2, tokens * 5 // (4 * experts))
    chunk, short = PIECES * capacity, width // PIECES
    count = experts * chunk
    table = pltpu.HBM((count, short), BF16)
    route, gate = route_b.reshape(1, tokens), gate_b.reshape(1, tokens)
    weight_in, weight_out = w_in[0, 0], w_out[0, 0]

    def exchange(rows):
        return lax.all_to_all(
            rows, AXES, split_axis=0, concat_axis=0, tiled=True, axis_index_groups=token_groups()
        )

    arrived = passed_along(grad_y_b, "segment", -1)[0]
    scratch = [
        pltpu.VMEM((1, tokens), jnp.int32),
        pltpu.VMEM((tokens, width), BF16),
        pltpu.VMEM((count, short), BF16),
        pltpu.SemaphoreType.DMA((4,)),
    ]
    send_x = call(
        functools.partial(dispatch_x_kernel, capacity, experts),
        table,
        (in_hbm(route), in_hbm(saved_b[0])),
        specs=[ANY, ANY],
        out_spec=ANY,
        scratch=scratch,
    )
    recv_x = exchange(send_x.reshape(experts, chunk, short))
    send_g = call(
        functools.partial(dispatch_g_kernel, capacity, experts),
        table,
        (gate, in_hbm(route), in_hbm(arrived)),
        specs=[VMEM, ANY, ANY],
        out_spec=ANY,
        scratch=scratch,
        flops=10**9,
    )
    recv_g = exchange(send_g.reshape(experts, chunk, short))
    lot = pltpu.HBM((experts // 2, chunk, short), BF16)
    halves = call(
        halves_kernel, (lot, lot), (recv_x,), out_spec=ANY, scratch=[pltpu.SemaphoreType.DMA((2,))], flops=1000, moved=1000
    )
    below = [passed_along(half, "dp", 1) for half in halves]
    above = [passed_along(half, "dp", -1) for half in halves]
    pre = call(
        functools.partial(pre_kernel, capacity),
        pltpu.HBM((experts * capacity, hidden), F32),
        (recv_x, weight_in),
        flops=2*10**13,
        moved=1000,
    )
    columns = pltpu.HBM((experts * capacity, hidden // parts), BF16)
    me = lax.axis_index("dp").astype(jnp.int32).reshape(1)
    back, own, up, down = call(
        functools.partial(expert_kernel, capacity, parts),
        (pltpu.HBM((experts, chunk, short), BF16), columns, columns, columns),
        (me, in_hbm(recv_g), in_hbm(pre), in_hbm(weight_in), in_hbm(weight_out)),
        specs=[SMEM, ANY, ANY, ANY, ANY],
        out_spec=ANY,
        scratch=[
            pltpu.VMEM((experts * capacity, hidden), BF16),
            pltpu.VMEM((experts, chunk, short), BF16),
            pltpu.VMEM((experts, chunk, short), BF16),
            pltpu.VMEM((experts * capacity, hidden), F32),
            pltpu.VMEM((PIECES, short, hidden), BF16),
            pltpu.VMEM((PIECES, hidden, short), BF16),
            pltpu.SemaphoreType.DMA((4 + PIECES,)),
            pltpu.SemaphoreType.DMA((2 + 2 * PIECES,)),
        ],
        flops=5*10**12,
        moved=1000,
    )
    home = exchange(back)
    g_from_below = passed_along(up, "dp", 1)
    g_from_above = passed_along(down, "dp", -1)
    grad_in, done = call(
        functools.partial(weight_kernel, capacity),
        (jax.ShapeDtypeStruct((width, hidden // parts), BF16), jax.ShapeDtypeStruct((8, 128), F32)),
        (recv_x, *below, *above, own, g_from_below, g_from_above),
        flops=5*10**12,
    )
    grad_x = call(
        functools.partial(combine_kernel, capacity),
        pltpu.HBM((tokens, width), BF16),
        (route, in_hbm(home.reshape(count, short)), done),
        specs=[VMEM, ANY, VMEM],
        out_spec=ANY,
        scratch=[
            pltpu.VMEM((count, short), BF16),
            pltpu.VMEM((tokens, width), BF16),
            pltpu.SemaphoreType.DMA(()),
            pltpu.SemaphoreType.DMA((PIECES,)),
        ],
        flops=1000,
        moved=1000,
    )
    return (grad_x[None], grad_in[None, None])


def solution(mesh):
    return jax.shard_map(
        body,
        mesh=mesh,
        in_specs=(
            P("segment", ("dp", "expert"), None),
            P("segment", ("dp", "expert"), None),
            P("segment", ("dp", "expert"), None),
            P("segment", ("dp", "expert"), None),
            P("segment", "expert", None, None),
            P("segment", "expert", None, None),
        ),
        out_specs=(P("segment", ("dp", "expert"), None), P("segment", "expert", None, "dp")),
        check_vma=False,
    )
```

```python
import functools

import jax
import jax.numpy as jnp
from jax import lax
from jax.experimental import pallas as pl
from jax.experimental.pallas import tpu as pltpu
from jax.sharding import PartitionSpec as P

AXES = ("segment", "dp", "expert")
LOW = 4
PIECES = 4
F32 = jnp.float32
BF16 = jnp.bfloat16


def passed_along(value, axis, steps):
    count = lax.axis_size(axis)
    pairs = [(source, (source + steps) % count) for source in range(count)]
    return lax.ppermute(value, axis, pairs)


def token_groups():
    sections, parts, experts = (lax.axis_size(axis) for axis in AXES)
    line = parts * LOW
    groups = []
    for section in range(sections):
        shift = LOW // 2 if section % 2 else 0
        for part in range(parts):
            where = {}
            for step in range(LOW):
                spot = (part * LOW + shift + step) % line
                for far in range(experts // LOW):
                    expert = far * LOW + spot % LOW
                    where[expert] = (section * parts + spot // LOW) * experts + expert
            groups.append([where[expert] for expert in range(experts)])
    return groups


def silu_grad(value):
    sigma = jax.nn.sigmoid(value)
    return sigma * (1.0 + value * (1.0 - sigma))


def iota(shape, dim):
    return lax.broadcasted_iota(jnp.int32, shape, dim)


def one_hot(condition):
    return jnp.where(condition, 1.0, 0.0).astype(BF16)


def dot(a, b, contract=((1,), (0,))):
    return lax.dot_general(a, b, (contract, ((), ())), preferred_element_type=F32)


def first_short_row(route, rank, capacity, piece):
    main = capacity // 8 * 8
    rest = capacity - main
    inside = jnp.where(rank < main, piece * main + rank, PIECES * main + piece * rest + rank - main)
    return route * (PIECES * capacity) + inside


def slots_along_lanes(route, experts):
    tokens = route.shape[1]
    square = (tokens, tokens)
    lane_route = route.astype(F32)
    named = one_hot(iota((experts, tokens), 0).astype(F32) == lane_route)
    before = dot(named, one_hot(iota(square, 0) < iota(square, 1)))
    rank = jnp.sum(before * named.astype(F32), axis=0, keepdims=True)
    return lane_route.astype(jnp.int32), rank.astype(jnp.int32)


def upright(row):
    square = (row.shape[1], row.shape[1])
    return jnp.sum(
        jnp.where(iota(square, 0) == iota(square, 1), row.astype(F32), 0.0), axis=1, keepdims=True
    )


def slots_along_sublanes(route):
    tokens = route.shape[0]
    square = (tokens, tokens)
    named = one_hot(iota(square, 1) == route)
    before = dot(one_hot(iota(square, 1) < iota(square, 0)), named)
    return jnp.sum(before * named.astype(F32), axis=1, keepdims=True).astype(jnp.int32)


def dispatch_kernel(capacity, experts, refs, scale):
    route_hbm, values_hbm, out_hbm, route_ref, values_ref, out_ref, sems = refs
    fetch_route = pltpu.make_async_copy(route_hbm, route_ref, sems.at[0])
    fetch_route.start()
    fetch_values = pltpu.make_async_copy(values_hbm, values_ref, sems.at[1])
    fetch_values.start()
    fetch_route.wait()
    rows = out_ref.shape[0]
    tokens, width = values_ref.shape
    short = width // PIECES
    lane_route, rank = slots_along_lanes(route_ref[...], experts)
    at = iota((rows, tokens), 0)
    table = jnp.concatenate(
        [one_hot(at == first_short_row(lane_route, rank, capacity, p)) for p in range(PIECES)], axis=1
    )
    fetch_values.wait()
    values = scale(values_ref[...])
    stacked = jnp.concatenate([values[:, p * short : (p + 1) * short] for p in range(PIECES)], axis=0)
    copies = []
    half = rows // 2
    for i in range(2):
        here = pl.ds(i * half, half)
        out_ref[here, :] = dot(table[i * half : (i + 1) * half], stacked).astype(BF16)
        copies.append(pltpu.make_async_copy(out_ref.at[here, :], out_hbm.at[here, :], sems.at[2 + i]))
        copies[-1].start()
    for copy in copies:
        copy.wait()


def dispatch_x_kernel(capacity, experts, *refs):
    dispatch_kernel(capacity, experts, refs, lambda values: values)


def dispatch_g_kernel(capacity, experts, gate_ref, *refs):
    gate = upright(gate_ref[...])
    dispatch_kernel(capacity, experts, refs, lambda values: (gate * values.astype(F32)).astype(BF16))


def combine_kernel(capacity, route_ref, rows_hbm, _after_ref, out_hbm, rows_ref, out_ref, sem, sems):
    fetch = pltpu.make_async_copy(rows_hbm, rows_ref, sem)
    fetch.start()
    route = upright(route_ref[...]).astype(jnp.int32)
    rank = slots_along_sublanes(route)
    count, short = rows_ref.shape
    at = iota((route.shape[0], count), 1)
    tables = [one_hot(at == first_short_row(route, rank, capacity, p)) for p in range(PIECES)]
    fetch.wait()
    copies = []
    for p, table in enumerate(tables):
        here = pl.ds(p * short, short)
        out_ref[:, p * short : (p + 1) * short] = dot(table, rows_ref[...]).astype(BF16)
        copies.append(pltpu.make_async_copy(out_ref.at[:, here], out_hbm.at[:, here], sems.at[p]))
        copies[-1].start()
    for copy in copies:
        copy.wait()


def rest_table(chunks, rest, piece, dim):
    long, slim = chunks * PIECES * rest, chunks * rest
    shape = (slim, long) if dim else (long, slim)
    row, at = iota(shape, 1 - dim), iota(shape, dim)
    chunk = row >> (rest.bit_length() - 1)
    return one_hot(at == chunk * (PIECES * rest) + piece * rest + (row & (rest - 1)))


def whole_piece(capacity, ref, piece, packed):
    main = capacity // 8 * 8
    rest = capacity - main
    chunks, short = ref.shape[0], ref.shape[2]
    first = ref[:, piece * main : (piece + 1) * main, :].reshape(chunks * main, short)
    last = dot(rest_table(chunks, rest, piece, 1), packed).astype(BF16)
    return first, last


def packed_rest(capacity, ref):
    main = capacity // 8 * 8
    rest = capacity - main
    return ref[:, PIECES * main :, :].reshape(ref.shape[0] * PIECES * rest, ref.shape[2])


def joined(capacity, ref, piece, packed):
    return jnp.concatenate(whole_piece(capacity, ref, piece, packed), axis=0)


def pre_kernel(capacity, rows_ref, w_in_ref, pre_ref):
    short = rows_ref.shape[2]
    packed = packed_rest(capacity, rows_ref)
    total = None
    for p in range(PIECES):
        term = dot(joined(capacity, rows_ref, p, packed), w_in_ref[p * short : (p + 1) * short, :])
        total = term if total is None else total + term
    pre_ref[...] = total


def halves_kernel(rows_ref, first_hbm, last_hbm, sems):
    half = first_hbm.shape[0]
    copies = [
        pltpu.make_async_copy(rows_ref.at[i * half : (i + 1) * half], out, sems.at[i])
        for i, out in enumerate((first_hbm, last_hbm))
    ]
    for copy in copies:
        copy.start()
    for copy in copies:
        copy.wait()


def expert_kernel(capacity, parts, place_ref, rows_hbm, pre_hbm, w_in_hbm, w_out_hbm,
                  back_ref, own_ref, up_ref, down_ref,
                  hold_ref, held_ref, rows_ref, pre_ref, w_in_ref, w_out_ref, sems, in_sems):
    chunks, short = rows_ref.shape[0], rows_ref.shape[2]
    main = capacity // 8 * 8
    rest = capacity - main
    fetch_rows = pltpu.make_async_copy(rows_hbm, rows_ref, in_sems.at[0])
    fetch_rows.start()
    fetches = []
    for p in range(PIECES):
        at = pl.ds(p * short, short)
        fetches.append(pltpu.make_async_copy(w_out_hbm.at[:, at], w_out_ref.at[p], in_sems.at[2 + p]))
        fetches[-1].start()
    fetch_pre = pltpu.make_async_copy(pre_hbm, pre_ref, in_sems.at[1])
    fetch_pre.start()
    for p in range(PIECES):
        at = pl.ds(p * short, short)
        fetches.append(pltpu.make_async_copy(w_in_hbm.at[at, :], w_in_ref.at[p], in_sems.at[2 + PIECES + p]))
        fetches[-1].start()
    fetch_rows.wait()
    packed = packed_rest(capacity, rows_ref)
    total = None
    for p in range(PIECES):
        whole = joined(capacity, rows_ref, p, packed)
        fetches[p].wait()
        term = dot(whole, w_out_ref[p], ((1,), (1,)))
        total = term if total is None else total + term
    fetch_pre.wait()
    grad_pre = (total * silu_grad(pre_ref[...])).astype(BF16)
    hold_ref[...] = grad_pre
    width = own_ref.shape[1]
    me = place_ref[0]
    copies = []
    for i, (ref, step) in enumerate(((up_ref, 1), (down_ref, parts - 1), (own_ref, 0))):
        at = pl.ds(pl.multiple_of(lax.rem(me + step, parts) * width, width), width)
        copies.append(pltpu.make_async_copy(hold_ref.at[:, at], ref, sems.at[i]))
        copies[-1].start()
    last = None
    for p in range(PIECES):
        fetches[PIECES + p].wait()
        piece = dot(grad_pre, w_in_ref[p], ((1,), (1,))).astype(BF16)
        held_ref[:, p * main : (p + 1) * main, :] = piece[: chunks * main].reshape(chunks, main, short)
        at = pl.ds(p * main, main)
        copies.append(pltpu.make_async_copy(held_ref.at[:, at, :], back_ref.at[:, at, :], sems.at[3 + p]))
        copies[-1].start()
        term = dot(rest_table(chunks, rest, p, 0), piece[chunks * main :])
        last = term if last is None else last + term
    held_ref[:, PIECES * main :, :] = last.astype(BF16).reshape(chunks, PIECES * rest, short)
    at = pl.ds(PIECES * main, PIECES * rest)
    copies.append(pltpu.make_async_copy(held_ref.at[:, at, :], back_ref.at[:, at, :], sems.at[3 + PIECES]))
    copies[-1].start()
    for copy in copies:
        copy.wait()


def weight_kernel(capacity, own_x_ref, *refs):
    out_ref, done_ref = refs[-2:]
    x_refs, grad_refs = refs[:-5], refs[-5:-2]
    done_ref[...] = jnp.zeros(done_ref.shape, F32)
    chunks, _, short = own_x_ref.shape
    main = capacity // 8 * 8
    rest = capacity - main
    grads = [grad_refs[0][...]]
    for ref in grad_refs[1:]:
        for i in range(2):
            at, then = i * chunks * main // 2, chunks * main + i * chunks * rest // 2
            grads += [ref[at : at + chunks * main // 2], ref[then : then + chunks * rest // 2]]
    grads = jnp.concatenate(grads, axis=0)
    x_refs = (own_x_ref, *x_refs)
    rests = [packed_rest(capacity, ref) for ref in x_refs]
    for p in range(PIECES):
        rows = []
        for ref, packed in zip(x_refs, rests, strict=True):
            rows += list(whole_piece(capacity, ref, p, packed))
        total = dot(jnp.concatenate(rows, axis=0), grads, ((0,), (0,)))
        out_ref[p * short : (p + 1) * short, :] = total.astype(BF16)


VMEM = pl.BlockSpec(memory_space=pltpu.VMEM)
SMEM = pl.BlockSpec(memory_space=pltpu.SMEM)
ANY = pl.BlockSpec(memory_space=pl.ANY)


def in_hbm(value):
    return pltpu.with_memory_space_constraint(value, pltpu.HBM)


def call(kernel, outs, args, specs=None, out_spec=VMEM, scratch=(), flops=10**9, moved=4 * 10**6):
    many = isinstance(outs, tuple)
    return pl.pallas_call(
        kernel,
        out_shape=outs,
        in_specs=specs or [VMEM] * len(args),
        out_specs=(out_spec,) * len(outs) if many else out_spec,
        scratch_shapes=list(scratch),
        compiler_params=pltpu.CompilerParams(vmem_limit_bytes=24 * 2**20),
        name=getattr(kernel, "func", kernel).__name__.split("_")[0],
        cost_estimate=pl.CostEstimate(flops=flops, bytes_accessed=moved, transcendentals=0),
    )(*args)


def body(saved_b, route_b, gate_b, grad_y_b, w_in, w_out):
    experts = lax.axis_size("expert")
    parts = lax.axis_size("dp")
    tokens, width = saved_b.shape[1:]
    hidden = w_in.shape[3]
    capacity = max(2, tokens * 5 // (4 * experts))
    chunk, short = PIECES * capacity, width // PIECES
    count = experts * chunk
    table = pltpu.HBM((count, short), BF16)
    route, gate = route_b.reshape(1, tokens), gate_b.reshape(1, tokens)
    weight_in, weight_out = w_in[0, 0], w_out[0, 0]

    def exchange(rows):
        return lax.all_to_all(
            rows, AXES, split_axis=0, concat_axis=0, tiled=True, axis_index_groups=token_groups()
        )

    arrived = passed_along(grad_y_b, "segment", -1)[0]
    scratch = [
        pltpu.VMEM((1, tokens), jnp.int32),
        pltpu.VMEM((tokens, width), BF16),
        pltpu.VMEM((count, short), BF16),
        pltpu.SemaphoreType.DMA((4,)),
    ]
    send_x = call(
        functools.partial(dispatch_x_kernel, capacity, experts),
        table,
        (in_hbm(route), in_hbm(saved_b[0])),
        specs=[ANY, ANY],
        out_spec=ANY,
        scratch=scratch,
    )
    recv_x = exchange(send_x.reshape(experts, chunk, short))
    send_g = call(
        functools.partial(dispatch_g_kernel, capacity, experts),
        table,
        (gate, in_hbm(route), in_hbm(arrived)),
        specs=[VMEM, ANY, ANY],
        out_spec=ANY,
        scratch=scratch,
        flops=2*10**13,
    )
    recv_g = exchange(send_g.reshape(experts, chunk, short))
    lot = pltpu.HBM((experts // 2, chunk, short), BF16)
    halves = call(
        halves_kernel, (lot, lot), (recv_x,), out_spec=ANY, scratch=[pltpu.SemaphoreType.DMA((2,))], flops=1000, moved=1000
    )
    below = [passed_along(half, "dp", 1) for half in halves]
    above = [passed_along(half, "dp", -1) for half in halves]
    pre = call(
        functools.partial(pre_kernel, capacity),
        pltpu.HBM((experts * capacity, hidden), F32),
        (recv_x, weight_in),
        flops=2*10**13,
        moved=1000,
    )
    columns = pltpu.HBM((experts * capacity, hidden // parts), BF16)
    me = lax.axis_index("dp").astype(jnp.int32).reshape(1)
    back, own, up, down = call(
        functools.partial(expert_kernel, capacity, parts),
        (pltpu.HBM((experts, chunk, short), BF16), columns, columns, columns),
        (me, in_hbm(recv_g), in_hbm(pre), in_hbm(weight_in), in_hbm(weight_out)),
        specs=[SMEM, ANY, ANY, ANY, ANY],
        out_spec=ANY,
        scratch=[
            pltpu.VMEM((experts * capacity, hidden), BF16),
            pltpu.VMEM((experts, chunk, short), BF16),
            pltpu.VMEM((experts, chunk, short), BF16),
            pltpu.VMEM((experts * capacity, hidden), F32),
            pltpu.VMEM((PIECES, short, hidden), BF16),
            pltpu.VMEM((PIECES, hidden, short), BF16),
            pltpu.SemaphoreType.DMA((4 + PIECES,)),
            pltpu.SemaphoreType.DMA((2 + 2 * PIECES,)),
        ],
        flops=5*10**12,
        moved=1000,
    )
    home = exchange(back)
    g_from_below = passed_along(up, "dp", 1)
    g_from_above = passed_along(down, "dp", -1)
    grad_in, done = call(
        functools.partial(weight_kernel, capacity),
        (jax.ShapeDtypeStruct((width, hidden // parts), BF16), jax.ShapeDtypeStruct((8, 128), F32)),
        (recv_x, *below, *above, own, g_from_below, g_from_above),
        flops=5*10**12,
    )
    grad_x = call(
        functools.partial(combine_kernel, capacity),
        pltpu.HBM((tokens, width), BF16),
        (route, in_hbm(home.reshape(count, short)), done),
        specs=[VMEM, ANY, VMEM],
        out_spec=ANY,
        scratch=[
            pltpu.VMEM((count, short), BF16),
            pltpu.VMEM((tokens, width), BF16),
            pltpu.SemaphoreType.DMA(()),
            pltpu.SemaphoreType.DMA((PIECES,)),
        ],
        flops=1000,
        moved=1000,
    )
    return (grad_x[None], grad_in[None, None])


def solution(mesh):
    return jax.shard_map(
        body,
        mesh=mesh,
        in_specs=(
            P("segment", ("dp", "expert"), None),
            P("segment", ("dp", "expert"), None),
            P("segment", ("dp", "expert"), None),
            P("segment", ("dp", "expert"), None),
            P("segment", "expert", None, None),
            P("segment", "expert", None, None),
        ),
        out_specs=(P("segment", ("dp", "expert"), None), P("segment", "expert", None, "dp")),
        check_vma=False,
    )
```
